128 devices in a mesh: lat: 8 (over x_hi, y), ang: 16 (over x_lo, z, core).
Axes of the slice: x: 4 (x_hi: 2, x_lo: 2; x = x_hi * 2 + x_lo), y: 4, z: 4, core: 2. Of those that a mesh axis runs over, the one named last changes fastest.
Arguments:
- incident: float32 [2, 256, 262144], P(None, 'ang', 'lat'), may hold values from -6 to 6
- detuning: float32 [256], P('ang'), may hold values from -1.5 to 1.5
- phase_table: int32 [3, 262144], P(None, 'lat'), may hold values from -32768 to 32767
- response: float32 [256, 256], replicated, may hold values from 0 to 2, as said below
- counts: int32 [256, 262144], P(None, ('lat', 'ang')), may hold values from 0 to 3
Outputs:
- exit_field: float32 [2, 256, 262144], P(None, 'ang', 'lat')
- estimate: float32 [256, 262144], P('ang', 'lat')
The draws below stay inside these ranges and needn't reach their ends.
Inputs may be any that keep to these rules, and one draw needn't show every extreme that they name: `response`: every entry is positive.
All inputs are finite; a program needn't handle non-finite values.
Results may differ from the reference program's by a relative error of at most 0.00013.
Values sent between devices are 32-bit elements; how exact they have to be, the bound alone decides.
No kernel may reach another device: no remote copies, remote signals or barrier semaphores. Data moves between devices by JAX's collectives and lax.ppermute only.
A program may use at most 64 MiB of HBM per device.

```python
import math
import jax
import jax.numpy as jnp
from jax import lax

COLS = 512
ANGLES = 256
BLOCKS = 3
STEPS = 3
ITERS = 6
NPOINTS = 262144


def draw_response(key, part):
    key_diagonal = jax.random.fold_in(key, 11)
    key_band = jax.random.fold_in(key, 12)
    band_width = ANGLES // 8
    angle_index = jnp.arange(ANGLES)
    distance = jnp.abs(angle_index[:, None] - angle_index[None, :]).astype(jnp.float32)
    roughness = jax.random.uniform(key_band, (ANGLES, ANGLES), jnp.float32, 0.05, 1.0)
    diagonal_part = jax.random.uniform(key_diagonal, (ANGLES,), jnp.float32, 0.3, 0.6)
    banded = roughness * jnp.exp(-distance / band_width) * (0.5 / band_width)
    return banded + jnp.diag(diagonal_part)


def place_ends(result, stream_key, low, high):
    index_at = [jax.random.randint(jax.random.fold_in(stream_key, axis), (), 0, length) for axis, length in enumerate(result.shape)]
    main_axis = result.shape.index(max(result.shape))
    neighbour = index_at[:main_axis] + [(index_at[main_axis] + 1) % result.shape[main_axis]] + index_at[main_axis + 1:]
    return result.at[tuple(index_at)].set(low).at[tuple(neighbour)].set(high)


def block_scale(key, dims, split, least, largest):
    level, own = 1.0, jax.random.fold_in(key, 6)
    for position, parts in split:
        steps = jnp.exp(jax.random.uniform(jax.random.fold_in(own, position), (parts,), jnp.float32, least / len(split), largest / len(split)))
        level = level * jnp.repeat(steps, dims[position] // parts).reshape([-1 if axis == position else 1 for axis in range(len(dims))])
    return level


def scatter_about(stream_key, extent, deviation, reach, pieces=(), held_as=jnp.bfloat16):
    values = jax.random.normal(stream_key, extent, jnp.float32) * deviation
    if len(pieces) > 0:
        values = block_scale(stream_key, extent, pieces, -0.22, 0.18) * values
    return jnp.clip(values, min=-reach, max=reach).astype(held_as)


def setup_inputs(seed: int = 0) -> dict:
    key_list = jax.random.split(jax.random.key(seed), 6)
    incident = scatter_about(key_list[0], (2, ANGLES, NPOINTS), 1.0, 6.0, ((1, 16), (2, 8)), jnp.float32)
    detuning = jnp.clip(jax.random.uniform(key_list[1], (ANGLES,), jnp.float32, -1.5, 1.5) * block_scale(key_list[1], (ANGLES,), ((0, 16),), -0.4, 0.0), -1.5, 1.5)
    phase_table = place_ends(jax.random.randint(key_list[2], (BLOCKS, NPOINTS), -32768, 32768), jax.random.fold_in(key_list[2], 1), -32768, 32767).astype(jnp.int32)
    response = draw_response(jax.random.fold_in(key_list[5], 71), 0)
    counts = place_ends(jax.random.randint(key_list[4], (ANGLES, NPOINTS), 0, 4), jax.random.fold_in(key_list[4], 1), 0, 3).astype(jnp.int32)
    return dict(incident=incident, detuning=detuning, phase_table=phase_table, response=response, counts=counts)


coupling = 0.6
background = 0.25
phase_unit = math.pi / 32768.0


def rotate(beam_real, beam_imag, bragg_real, bragg_imag, phase_cos, phase_sin, detune_cos, detune_sin):
    cos_kappa = math.cos(coupling)
    sin_kappa = math.sin(coupling)
    mixed_real = phase_cos * bragg_real + phase_sin * bragg_imag
    mixed_imag = phase_cos * bragg_imag - phase_sin * bragg_real
    ahead_real = cos_kappa * beam_real - sin_kappa * mixed_imag
    ahead_imag = cos_kappa * beam_imag + sin_kappa * mixed_real
    driven_real = phase_cos * beam_real - phase_sin * beam_imag
    driven_imag = phase_cos * beam_imag + phase_sin * beam_real
    inner_real = cos_kappa * bragg_real - sin_kappa * driven_imag
    inner_imag = cos_kappa * bragg_imag + sin_kappa * driven_real
    out_real = detune_cos * inner_real + detune_sin * inner_imag
    out_imag = detune_cos * inner_imag - detune_sin * inner_real
    return ahead_real, ahead_imag, out_real, out_imag


def reference(incident, detuning, phase_table, response, counts):
    detune_cos = jnp.cos(detuning)[:, None]
    detune_sin = jnp.sin(detuning)[:, None]
    beam_real = incident[0]
    beam_imag = incident[1]
    bragg_real = jnp.zeros_like(beam_real)
    bragg_imag = jnp.zeros_like(beam_real)
    for block_index in range(BLOCKS):
        phase_angle = phase_table[block_index].astype(jnp.float32) * phase_unit
        phase_cos = jnp.cos(phase_angle)[None, :]
        phase_sin = jnp.sin(phase_angle)[None, :]
        for step_index in range(STEPS):
            turned = rotate(beam_real, beam_imag, bragg_real, bragg_imag, phase_cos, phase_sin, detune_cos, detune_sin)
            beam_real = jnp.roll(turned[0], COLS, axis=1)
            beam_imag = jnp.roll(turned[1], COLS, axis=1)
            bragg_real = jnp.roll(turned[2], -COLS, axis=1)
            bragg_imag = jnp.roll(turned[3], -COLS, axis=1)
    exit_field = jnp.stack([bragg_real, bragg_imag])
    estimate = bragg_real * bragg_real + bragg_imag * bragg_imag
    measured = counts.astype(jnp.float32)
    column_sums = jnp.sum(response, axis=0)[:, None]
    for iteration in range(ITERS):
        blurred = jnp.dot(response, estimate, precision=lax.Precision.HIGHEST, preferred_element_type=jnp.float32) + background
        projected = lax.dot_general(response, measured / blurred, (((0,), (0,)), ((), ())), precision=lax.Precision.HIGHEST, preferred_element_type=jnp.float32)
        estimate = estimate * projected / column_sums
    return exit_field, estimate
```

```python
import functools
import math

import jax
import jax.numpy as jnp
from jax import lax
from jax.experimental import pallas as pl
from jax.experimental.pallas import tpu as pltpu
from jax.sharding import PartitionSpec as P


COLS = 512
ITERS = 6
W = 256
CHUNKS = COLS // W
TILES = W // 128
BELOW, ABOVE = 7, 9

coupling = 0.6
background = 0.25
TAN2 = math.tan(coupling) ** 2
SCALE = math.cos(coupling) ** 9 / math.tan(coupling)
TABLE_OF_STEP = (0, 0, 1, 2, 2, 3, 4, 4)


def passed_along(x, axis, by):
    devices = lax.axis_size(axis)
    return lax.ppermute(x, axis, [(i, (i + by) % devices) for i in range(devices)])


def turn(units):
    u = units * (1.0 / 32768.0)
    q = u * u
    half = math.pi / 2
    s = (-1) ** 5 * half**11 / math.factorial(11)
    for k in (4, 3, 2, 1, 0):
        s = s * q + (-1) ** k * half ** (2 * k + 1) / math.factorial(2 * k + 1)
    s = s * u
    c = half**12 / math.factorial(12)
    for k in (5, 4, 3, 2, 1, 0):
        c = c * q + (-1) ** k * half ** (2 * k) / math.factorial(2 * k)
    return 1.0 - 2.0 * s * s, 2.0 * s * c


def times(ar, ai, br, bi):
    return ar * br - ai * bi, ar * bi + ai * br


def in_hbm(x):
    return pltpu.with_memory_space_constraint(x, pltpu.HBM)


def pack_kernel(rows, incident, phase, *refs):
    outs, edge, sems, edge_sems = refs[:-3], refs[-3], refs[-2], refs[-1]
    sides = ((rows - BELOW, BELOW), (0, ABOVE))
    edges = [
        pltpu.make_async_copy(
            phase.at[:, first * COLS : (first + count) * COLS], edge.at[side, :, 0 : count * COLS], edge_sems.at[side]
        )
        for side, (first, count) in enumerate(sides)
    ]
    for c in edges:
        c.start()
    copies = []
    for chunk in range(CHUNKS):
        for side, (first, count) in enumerate(sides):
            out = outs[2 * chunk + side]
            for i in range(count):
                at = (first + i) * COLS + chunk * W
                for part in range(2):
                    copies.append(
                        pltpu.make_async_copy(
                            incident.at[part, :, at : at + W],
                            out.at[16 * part : 16 * part + 16, i * W : i * W + W],
                            sems.at[chunk, side, i, part],
                        )
                    )
                    copies[-1].start()
    for c in edges:
        c.wait()
    for chunk in range(CHUNKS):
        for side, (first, count) in enumerate(sides):
            out = outs[2 * chunk + side]
            for t in range(TILES):
                at = count * W + t * 128
                out[:, at : at + 128] = jnp.zeros((32, 128), jnp.float32)
                for i in range(count):
                    lane = i * COLS + chunk * W + t * 128
                    out[3 * i : 3 * i + 3, at : at + 128] = edge[side, :, lane : lane + 128].astype(jnp.float32)
    for c in copies:
        c.wait()


def pack(incident, phase):
    rows = incident.shape[2] // COLS
    widths = [BELOW * W + TILES * 128, ABOVE * W + TILES * 128] * CHUNKS
    return pl.pallas_call(
        functools.partial(pack_kernel, rows),
        out_shape=tuple(jax.ShapeDtypeStruct((32, w), jnp.float32) for w in widths),
        in_specs=[pl.BlockSpec(memory_space=pl.ANY)] * 2,
        out_specs=(pl.BlockSpec(memory_space=pltpu.VMEM),) * len(widths),
        scratch_shapes=[
            pltpu.VMEM((2, 3, ABOVE * COLS), jnp.int32),
            pltpu.SemaphoreType.DMA((CHUNKS, 2, ABOVE, 2)),
            pltpu.SemaphoreType.DMA((2,)),
        ],
        compiler_params=pltpu.CompilerParams(vmem_limit_bytes=8 * 1024 * 1024),
        cost_estimate=pl.CostEstimate(flops=0, bytes_accessed=2 * 1024 * 1024, transcendentals=0),
        name="pack",
    )(in_hbm(incident), in_hbm(phase))


PARTS = {
    "inner": ((0, 48),),
    "border": ((-8, 8), (47, 10)),
    "whole": ((-7, 64),),
}
OWN_ROWS = {"inner": ((0, 64),), "border": ((0, 16), (47, 64)), "whole": ((0, 64),)}
OWN_PHASES = {"inner": ((0, 64),), "border": ((0, 16), (40, 64)), "whole": ((0, 64),)}
TABLE_ROWS = {"inner": ((1, 9),), "border": ((0, 3), (6, 11)), "whole": ((0, 11),)}


def advance_gauge(gauge_in, gauge):
    step = gauge_in[8, 0], gauge_in[8, 1]
    strands = []
    for k in range(8):
        strands += [gauge_in[k, 0], gauge_in[k, 1]]
        gauge[k, 0] = strands[-2]
        gauge[k, 1] = strands[-1]

    def advance(i, strands):
        ahead = []
        for k in range(8):
            gr, gi = times(strands[2 * k], strands[2 * k + 1], *step)
            gauge[8 * i + 8 + k, 0] = gr
            gauge[8 * i + 8 + k, 1] = gi
            ahead += [gr, gi]
        return tuple(ahead)

    lax.fori_loop(0, 10, advance, tuple(strands))


def sweep_kernel(mode, chunk, incident, phase, gauge_in, *refs):
    below = above = inner_inten = stage = None
    if mode != "inner":
        below, above, refs = refs[0], refs[1], refs[2:]
    if mode == "border":
        inner_inten, refs = refs[0], refs[1:]
    raw_out, inten_out, last_out, own, wave, phases, tab, last, gauge, raw, stage, sems = refs
    arrivals = [
        pltpu.make_async_copy(incident.at[:, :, lo * COLS : hi * COLS], own.at[:, :, lo * COLS : hi * COLS], sems.at[k])
        for k, (lo, hi) in enumerate(OWN_ROWS[mode])
    ]
    for c in arrivals:
        c.start()
    advance_gauge(gauge_in, gauge)

    for t in range(TILES):
        for lo, hi in OWN_PHASES[mode]:
            for r in range(lo, hi):
                lane = r * COLS + chunk * W + t * 128
                units = phase[:, lane : lane + 128].astype(jnp.float32)
                for b in range(3):
                    phases[b, t, r + 8 : r + 9, :] = units[b : b + 1]
        if mode != "inner":
            for ref, count, first in ((below, BELOW, 1), (above, ABOVE, 72)):
                lanes = slice(count * W + t * 128, count * W + t * 128 + 128)
                for i in range(count):
                    for b in range(3):
                        phases[b, t, first + i : first + i + 1, :] = ref[3 * i + b : 3 * i + b + 1, lanes]

    top_row = lax.broadcasted_iota(jnp.int32, (8, 128), 0) == 0

    def tables(j, carried):
        at = pl.multiple_of(8 * j, 8)
        rolled = []
        for t in range(TILES):
            here, before = [], []
            for b in range(3):
                here.append(turn(phases[b, t, pl.ds(at, 8), :]))
                pair = []
                for q in range(2):
                    r = pltpu.roll(here[b][q], 1, 0)
                    pair.append(jnp.where(top_row, carried[(t * 3 + b) * 2 + q], r))
                    rolled.append(r)
                before.append(pair)
            for k, (a, b) in enumerate(((0, 0), (0, 1), (1, 1), (1, 2), (2, 2))):
                br, bi = before[b]
                ar, ai = here[a]
                tab[k, 0, t, pl.ds(at, 8), :] = ar * br + ai * bi
                tab[k, 1, t, pl.ds(at, 8), :] = ai * br - ar * bi
            last[0, t, pl.ds(at, 8), :] = SCALE * here[2][1]
            last[1, t, pl.ds(at, 8), :] = -SCALE * here[2][0]
        return tuple(rolled)

    for lo, hi in TABLE_ROWS[mode]:
        lax.fori_loop(lo, hi, tables, (jnp.zeros((8, 128), jnp.float32),) * (6 * TILES))
    departures = [pltpu.make_async_copy(last, last_out, sems.at[2])]
    departures[0].start()

    def regauge(row, at, re_of, im_of):
        er, ei = gauge[row + 10, 0], gauge[row + 10, 1]
        for t in range(TILES):
            tr, ti = times(re_of(t), im_of(t), er, ei)
            wave[at, 0, :, t * 128 : t * 128 + 128] = tr
            wave[at, 1, :, t * 128 : t * 128 + 128] = ti

    def packet(r0, low, place, tile, state, steps):
        lanes = pl.ds(pl.multiple_of(tile * 128, 128), 128)
        tr = wave[r0 - low, 0, :, lanes]
        ti = wave[r0 - low, 1, :, lanes]
        after = []
        for n in range(steps):
            if n == 0:
                nr, ni = -TAN2 * tr, -TAN2 * ti
            else:
                dr, di = state[2 * n - 2], state[2 * n - 1]
                nr, ni = dr - TAN2 * tr, di - TAN2 * ti
                if n < steps - 1:
                    tr, ti = tr + dr, ti + di
            if n < 8:
                k = TABLE_OF_STEP[n]
                hr = tab[k, 0, tile, pl.ds(r0 + n + 8, 1), :]
                hi = tab[k, 1, tile, pl.ds(r0 + n + 8, 1), :]
                after += times(nr, ni, hr, hi)
        if steps == 9:
            raw[tile, place + r0 - low, 0] = nr
            raw[tile, place + r0 - low, 1] = ni
            inten = SCALE * SCALE * (nr * nr + ni * ni)
            if mode == "inner":
                inten_out[r0 - low, :, lanes] = inten
            elif mode == "border":
                stage[place + r0 - low, :, lanes] = inten
            else:
                row = r0 + 7
                off = pl.multiple_of((row % 4) * W + tile * 128, 128)
                inten_out[row // 4, :, pl.ds(off, 128)] = inten
        return tuple(after)

    for c in arrivals:
        c.wait()
    place = 0
    for low, count in PARTS[mode]:
        high = low + count + 15
        if low < 0:
            for i in range(BELOW):
                lanes = lambda t, i=i: slice(i * W + t * 128, i * W + t * 128 + 128)
                regauge(i - BELOW, i - BELOW - low, lambda t: below[0:16, lanes(t)], lambda t: below[16:32, lanes(t)])
        if high > 64:
            for i in range(ABOVE):
                lanes = lambda t, i=i: slice(i * W + t * 128, i * W + t * 128 + 128)
                regauge(64 + i, 64 + i - low, lambda t: above[0:16, lanes(t)], lambda t: above[16:32, lanes(t)])

        def own_row(row, low=low):
            lanes = lambda t: pl.ds(pl.multiple_of(row * COLS + chunk * W + t * 128, 128), 128)
            regauge(row, row - low, lambda t: own[0, :, lanes(t)], lambda t: own[1, :, lanes(t)])

        first, end = max(low, 0), min(high, 63) + 1
        fours = (end - first) // 4

        @pl.loop(0, fours)
        def _(j, first=first, own_row=own_row):
            for k in range(4):
                own_row(first + 4 * j + k)

        for row in range(first + 4 * fours, end):
            own_row(row)

        @pl.loop(0, TILES)
        def _(tile, low=low, high=high, count=count, place=place):
            @pl.loop(0, 2)
            def _(odd):
                top = high - odd
                state = ()
                for i in range(8):
                    state = packet(top - 2 * i, low, place, tile, state, i + 1)
                group = 5 if count == 10 else 4

                def several(j, state):
                    for i in range(group):
                        state = packet(top - 16 - 2 * group * j - 2 * i, low, place, tile, state, 9)
                    return state

                lax.fori_loop(0, count // 2 // group, several, state)

            if mode != "border":
                pltpu.make_async_copy(raw.at[tile], raw_out.at[tile], sems.at[3 + tile]).start()

        place += count
    if mode == "border":
        for tile in range(TILES):
            pltpu.make_async_copy(raw.at[tile], raw_out.at[tile], sems.at[3 + tile]).start()
        for row in range(64):
            if row < 7:
                value = stage[row + 1]
            elif row < 55:
                value = inner_inten[row - 7]
            else:
                value = stage[row - 46]
            inten_out[row // 4, :, (row % 4) * W : (row % 4) * W + W] = value
    departures[0].wait()
    for tile in range(TILES):
        pltpu.make_async_copy(raw.at[tile], raw_out.at[tile], sems.at[3 + tile]).wait()


def whole_block(shape):
    return pl.BlockSpec(shape, lambda i: (0,) * len(shape))


def sweep(mode, incident, phase, gauge, chunk, *more):
    total = sum(count for _, count in PARTS[mode])
    tall = max(count for _, count in PARTS[mode]) + 16
    shapes = ((TILES, total, 2, 16, 128), (48, 16, W) if mode == "inner" else (16, 16, 4 * W), (2, TILES, 88, 128))
    vmem, hbm = pl.BlockSpec(memory_space=pltpu.VMEM), pl.BlockSpec(memory_space=pltpu.HBM)
    return pl.pallas_call(
        functools.partial(sweep_kernel, mode, chunk),
        out_shape=(
            pltpu.HBM(shapes[0], jnp.float32),
            jax.ShapeDtypeStruct(shapes[1], jnp.float32),
            pltpu.HBM(shapes[2], jnp.float32),
        ),
        in_specs=[pl.BlockSpec(memory_space=pl.ANY)] + [vmem] * (2 + len(more)),
        out_specs=(hbm, vmem, hbm),
        scratch_shapes=[
            pltpu.VMEM(incident.shape, jnp.float32),
            pltpu.VMEM((tall, 2, 16, W), jnp.float32),
            pltpu.VMEM((3, TILES, 88, 128), jnp.float32),
            pltpu.VMEM((5, 2, TILES, 88, 128), jnp.float32),
            pltpu.VMEM((2, TILES, 88, 128), jnp.float32),
            pltpu.VMEM((88, 2, 16, 128), jnp.float32),
            pltpu.VMEM((TILES, total, 2, 16, 128), jnp.float32),
            pltpu.VMEM((18, 16, W), jnp.float32),
            pltpu.SemaphoreType.DMA((3 + TILES,)),
        ],
        compiler_params=pltpu.CompilerParams(vmem_limit_bytes=24 * 1024 * 1024),
        cost_estimate=pl.CostEstimate(flops=total * 16 * W * 120, bytes_accessed=8 * 1024 * 1024, transcendentals=0),
        name="sweep",
    )(in_hbm(incident), phase, gauge, *more)


def merge_kernel(gauge_in, inner, border, whole, last_inner, last_border, last_whole, out, gauge):
    advance_gauge(gauge_in, gauge)

    def put(row, chunk, ref, at, last):
        er, ei = gauge[row + 1, 0], gauge[row + 1, 1]
        for t in range(TILES):
            fr, fi = (last[q, t, pl.ds(row + 9, 1), :] for q in range(2))
            tr, ti = times(ref[t, at, 0], ref[t, at, 1], fr, fi)
            off = pl.multiple_of(row * COLS + chunk * W + t * 128, 128)
            out[0, :, pl.ds(off, 128)] = tr * er + ti * ei
            out[1, :, pl.ds(off, 128)] = ti * er - tr * ei

    @pl.loop(0, 24)
    def _(j):
        for k in range(2):
            put(2 * j + k + 7, 0, inner, 2 * j + k, last_inner)

    for row in range(7):
        put(row, 0, border, row + 1, last_border)
    for row in range(55, 64):
        put(row, 0, border, row - 46, last_border)

    @pl.loop(0, 32)
    def _(j):
        for k in range(2):
            put(2 * j + k, 1, whole, 2 * j + k, last_whole)


def merge(gauge, raws, lasts, span):
    return pl.pallas_call(
        merge_kernel,
        grid=(1,),
        out_shape=jax.ShapeDtypeStruct((2, 16, span), jnp.float32),
        in_specs=[whole_block(x.shape) for x in (gauge, *raws, *lasts)],
        out_specs=whole_block((2, 16, span)),
        scratch_shapes=[pltpu.VMEM((88, 2, 16, 128), jnp.float32)],
        cost_estimate=pl.CostEstimate(flops=0, bytes_accessed=8 * 1024 * 1024, transcendentals=0),
        name="merge",
    )(gauge, *raws, *lasts)


def place_kernel(chunk, block, *refs):
    out, sems = refs[-2:]
    copies = []
    for b in range(16):
        for r in range(4):
            at = (4 * b + r) * COLS + chunk * W
            copies.append(pltpu.make_async_copy(block.at[b, :, r * W : r * W + W], out.at[:, at : at + W], sems.at[b, r]))
            copies[-1].start()
    for c in copies:
        c.wait()


def place(block, chunk, span, onto=None):
    hbm = pl.BlockSpec(memory_space=pl.ANY)
    ops = [block] if onto is None else [block, onto]
    return pl.pallas_call(
        functools.partial(place_kernel, chunk),
        out_shape=jax.ShapeDtypeStruct((16, span), jnp.float32),
        in_specs=[pl.BlockSpec(memory_space=pltpu.VMEM)] + [hbm] * (len(ops) - 1),
        out_specs=hbm,
        scratch_shapes=[pltpu.SemaphoreType.DMA((16, 4))],
        input_output_aliases={} if onto is None else {1: 0},
        compiler_params=pltpu.CompilerParams(vmem_limit_bytes=4 * 1024 * 1024),
        cost_estimate=pl.CostEstimate(flops=0, bytes_accessed=4 * 1024 * 1024, transcendentals=0),
        name="place",
    )(*ops)


def deconvolve(estimate, response, scaled, measured):
    for _ in range(ITERS):
        blurred = jnp.dot(response, estimate, precision=lax.Precision.HIGH, preferred_element_type=jnp.float32) + background
        projected = lax.dot_general(
            scaled,
            measured / blurred,
            (((0,), (0,)), ((), ())),
            precision=lax.Precision.HIGH,
            preferred_element_type=jnp.float32,
        )
        estimate = estimate * projected
    return estimate


def exchange(x):
    return lax.all_to_all(x, "ang", split_axis=0, concat_axis=0, tiled=True)


def on_device(incident, detuning, phase_table, response, counts):
    span = incident.shape[2]
    edges = pack(incident, phase_table)
    below, above = [], []
    for chunk in range(CHUNKS):
        below.append(passed_along(edges[2 * chunk], "lat", 1))
        above.append(passed_along(edges[2 * chunk + 1], "lat", -1))
    angle = -0.5 * detuning[None, :] * jnp.array([-10.0, -9.0, -8.0, -7.0, -6.0, -5.0, -4.0, -3.0, 8.0], jnp.float32)[:, None]
    gauge = jnp.stack([jnp.cos(angle), jnp.sin(angle)], axis=1)
    gauge = jnp.broadcast_to(gauge[..., None], gauge.shape + (128,))

    column_sums = jnp.sum(response, axis=0)
    scaled = response / column_sums[None, :]
    measured = [
        jnp.concatenate([counts[:, r * COLS + c * W : r * COLS + c * W + W] for r in range(4)], axis=1).astype(jnp.float32)
        for c in range(CHUNKS)
    ]

    raw_inner, inten_inner, last_inner = sweep("inner", incident, phase_table, gauge, 0)
    raw_border, inten0, last_border = sweep("border", incident, phase_table, gauge, 0, below[0], above[0], inten_inner)
    there0 = exchange(inten0)
    raw_whole, inten1, last_whole = sweep("whole", incident, phase_table, gauge, 1, below[1], above[1])
    there1 = exchange(inten1)
    estimate0 = deconvolve(there0.reshape(256, 4 * W), response, scaled, measured[0])
    back0 = exchange(estimate0.reshape(16, 16, 4 * W))
    there1, estimate0 = lax.optimization_barrier((there1, estimate0))
    estimate1 = deconvolve(there1.reshape(256, 4 * W), response, scaled, measured[1])
    back1 = exchange(estimate1.reshape(16, 16, 4 * W))
    exit_field = merge(gauge, (raw_inner, raw_border, raw_whole), (last_inner, last_border, last_whole), span)
    result = place(back0, 0, span)
    result = place(back1, 1, span, result)
    return exit_field, result


def solution(mesh):
    return jax.shard_map(
        on_device,
        mesh=mesh,
        in_specs=(P(None, "ang", "lat"), P("ang"), P(None, "lat"), P(), P(None, ("lat", "ang"))),
        out_specs=(P(None, "ang", "lat"), P("ang", "lat")),
        check_vma=False,
    )
```

```python
import functools
import math

import jax
import jax.numpy as jnp
from jax import lax
from jax.experimental import pallas as pl
from jax.experimental.pallas import tpu as pltpu
from jax.sharding import PartitionSpec as P


COLS = 512
ITERS = 6
W = 256
CHUNKS = COLS // W
TILES = W // 128
BELOW, ABOVE = 7, 9

coupling = 0.6
background = 0.25
TAN2 = math.tan(coupling) ** 2
SCALE = math.cos(coupling) ** 9 / math.tan(coupling)
TABLE_OF_STEP = (0, 0, 1, 2, 2, 3, 4, 4)


def passed_along(x, axis, by):
    devices = lax.axis_size(axis)
    return lax.ppermute(x, axis, [(i, (i + by) % devices) for i in range(devices)])


def turn(units):
    u = units * (1.0 / 32768.0)
    q = u * u
    half = math.pi / 2
    s = (-1) ** 5 * half**11 / math.factorial(11)
    for k in (4, 3, 2, 1, 0):
        s = s * q + (-1) ** k * half ** (2 * k + 1) / math.factorial(2 * k + 1)
    s = s * u
    c = half**12 / math.factorial(12)
    for k in (5, 4, 3, 2, 1, 0):
        c = c * q + (-1) ** k * half ** (2 * k) / math.factorial(2 * k)
    return 1.0 - 2.0 * s * s, 2.0 * s * c


def times(ar, ai, br, bi):
    return ar * br - ai * bi, ar * bi + ai * br


def in_hbm(x):
    return pltpu.with_memory_space_constraint(x, pltpu.HBM)


def pack_kernel(incident, phase, *refs):
    outs, edge, sems, edge_sems = refs[:-3], refs[-3], refs[-2], refs[-1]
    rows = incident.shape[2] // COLS
    sides = ((rows - BELOW, BELOW), (0, ABOVE))
    edges = [
        pltpu.make_async_copy(
            phase.at[:, first * COLS : (first + count) * COLS], edge.at[side, :, 0 : count * COLS], edge_sems.at[side]
        )
        for side, (first, count) in enumerate(sides)
    ]
    for c in edges:
        c.start()
    copies = []
    for chunk in range(CHUNKS):
        for side, (first, count) in enumerate(sides):
            for i in range(count):
                at = (first + i) * COLS + chunk * W
                for part in range(2):
                    copies.append(
                        pltpu.make_async_copy(
                            incident.at[part, :, at : at + W],
                            outs[2 * chunk + side].at[16 * part : 16 * part + 16, i * W : i * W + W],
                            sems.at[chunk, side, i, part],
                        )
                    )
                    copies[-1].start()
    for c in edges:
        c.wait()
    for chunk in range(CHUNKS):
        for side, (first, count) in enumerate(sides):
            out = outs[2 * chunk + side]
            for t in range(TILES):
                at = count * W + t * 128
                out[:, at : at + 128] = jnp.zeros((32, 128), jnp.float32)
                for i in range(count):
                    lane = i * COLS + chunk * W + t * 128
                    out[3 * i : 3 * i + 3, at : at + 128] = edge[side, :, lane : lane + 128].astype(jnp.float32)
    for c in copies:
        c.wait()


def pack(incident, phase):
    widths = [BELOW * W + TILES * 128, ABOVE * W + TILES * 128] * CHUNKS
    return pl.pallas_call(
        pack_kernel,
        out_shape=tuple(jax.ShapeDtypeStruct((32, w), jnp.float32) for w in widths),
        in_specs=[pl.BlockSpec(memory_space=pl.ANY)] * 2,
        out_specs=(pl.BlockSpec(memory_space=pltpu.VMEM),) * len(widths),
        scratch_shapes=[
            pltpu.VMEM((2, 3, ABOVE * COLS), jnp.int32),
            pltpu.SemaphoreType.DMA((CHUNKS, 2, ABOVE, 2)),
            pltpu.SemaphoreType.DMA((2,)),
        ],
        compiler_params=pltpu.CompilerParams(vmem_limit_bytes=8 * 1024 * 1024),
        cost_estimate=pl.CostEstimate(flops=0, bytes_accessed=2 * 1024 * 1024, transcendentals=0),
        name="pack",
    )(in_hbm(incident), in_hbm(phase))


PARTS = {
    "inner": ((0, 48),),
    "border": ((-8, 8), (47, 10)),
    "whole": ((-7, 64),),
}
OWN_PHASES = {"inner": ((0, 64),), "border": ((0, 8), (48, 64)), "whole": ((0, 64),)}
TABLE_ROWS = {"inner": ((1, 9),), "border": ((0, 2), (8, 11)), "whole": ((0, 11),)}


def advance_gauge(gauge_in, gauge):
    step = gauge_in[8, 0], gauge_in[8, 1]
    strands = []
    for k in range(8):
        strands += [gauge_in[k, 0], gauge_in[k, 1]]
        gauge[k, 0] = strands[-2]
        gauge[k, 1] = strands[-1]

    def advance(i, strands):
        ahead = []
        for k in range(8):
            gr, gi = times(strands[2 * k], strands[2 * k + 1], *step)
            gauge[8 * i + 8 + k, 0] = gr
            gauge[8 * i + 8 + k, 1] = gi
            ahead += [gr, gi]
        return tuple(ahead)

    lax.fori_loop(0, 10, advance, tuple(strands))


def sweep_kernel(mode, chunk, phase, *refs):
    below = above = stage = state_out = None
    departures = []
    if mode == "border":
        below, above, inner_raw, inner_inten, state_in = refs[:5]
        inner_raw_out, raw_out, inten_out, last_out, tab, wave, gauge, phases, last, raw, stage, sems = refs[8:]
        departures = [
            pltpu.make_async_copy(inner_inten.at[2:13], inten_out.at[2:13], sems.at[0]),
            pltpu.make_async_copy(inner_raw, inner_raw_out, sems.at[1]),
        ]
        for c in departures:
            c.start()
    elif mode == "inner":
        incident, gauge_in, raw, inten_out, last_out, tab, wave, gauge, state_out, own, phases, last, sems = refs
    else:
        incident, gauge_in, below, above, raw_out, inten_out, last_out, tab, wave, gauge, own, phases, last, raw, sems = refs
    if mode != "border":
        half = incident.shape[2] // 2
        arrivals = [
            pltpu.make_async_copy(incident.at[:, :, k * half : k * half + half], own.at[:, :, k * half : k * half + half], sems.at[k])
            for k in range(2)
        ]
        for c in arrivals:
            c.start()
        advance_gauge(gauge_in, gauge)

    for t in range(TILES):
        for lo, hi in OWN_PHASES[mode]:
            for r in range(lo, hi):
                lane = r * COLS + chunk * W + t * 128
                units = phase[:, lane : lane + 128].astype(jnp.float32)
                for b in range(3):
                    phases[b, t, r + 8 : r + 9, :] = units[b : b + 1]
        if mode != "inner":
            for ref, count, first in ((below, BELOW, 1), (above, ABOVE, 72)):
                lanes = slice(count * W + t * 128, count * W + t * 128 + 128)
                for i in range(count):
                    for b in range(3):
                        phases[b, t, first + i : first + i + 1, :] = ref[3 * i + b : 3 * i + b + 1, lanes]

    top_row = lax.broadcasted_iota(jnp.int32, (8, 128), 0) == 0

    def tables(j, carried):
        at = pl.multiple_of(8 * j, 8)
        rolled = []
        for t in range(TILES):
            here, before = [], []
            for b in range(3):
                here.append(turn(phases[b, t, pl.ds(at, 8), :]))
                pair = []
                for q in range(2):
                    r = pltpu.roll(here[b][q], 1, 0)
                    pair.append(jnp.where(top_row, carried[(t * 3 + b) * 2 + q], r))
                    rolled.append(r)
                before.append(pair)
            for k, (a, b) in enumerate(((0, 0), (0, 1), (1, 1), (1, 2), (2, 2))):
                br, bi = before[b]
                ar, ai = here[a]
                tab[k, 0, t, pl.ds(at, 8), :] = ar * br + ai * bi
                tab[k, 1, t, pl.ds(at, 8), :] = ai * br - ar * bi
            last[0, t, pl.ds(at, 8), :] = SCALE * here[2][1]
            last[1, t, pl.ds(at, 8), :] = -SCALE * here[2][0]
        return tuple(rolled)

    for lo, hi in TABLE_ROWS[mode]:
        start = []
        for t in range(TILES):
            for b in range(3):
                if mode == "border" and lo > 0:
                    start += [pltpu.roll(x, 1, 0) for x in turn(phases[b, t, 8 * lo - 8 : 8 * lo, :])]
                else:
                    start += [jnp.zeros((8, 128), jnp.float32)] * 2
        lax.fori_loop(lo, hi, tables, tuple(start))
    departures.append(pltpu.make_async_copy(last, last_out, sems.at[2]))
    departures[-1].start()

    def regauge(row, re_of, im_of):
        er, ei = gauge[row + 10, 0], gauge[row + 10, 1]
        for t in range(TILES):
            tr, ti = times(re_of(t), im_of(t), er, ei)
            wave[row + 8, 0, :, t * 128 : t * 128 + 128] = tr
            wave[row + 8, 1, :, t * 128 : t * 128 + 128] = ti

    if mode != "inner":
        for ref, count, first in ((below, BELOW, -BELOW), (above, ABOVE, 64)):
            for i in range(count):
                lanes = lambda t, i=i: slice(i * W + t * 128, i * W + t * 128 + 128)
                regauge(first + i, lambda t, ref=ref: ref[0:16, lanes(t)], lambda t, ref=ref: ref[16:32, lanes(t)])
    if mode != "border":
        for c in arrivals:
            c.wait()

        @pl.loop(0, 16)
        def _(j):
            for k in range(4):
                row = 4 * j + k
                lanes = lambda t, row=row: pl.ds(pl.multiple_of(row * COLS + chunk * W + t * 128, 128), 128)
                regauge(row, lambda t: own[0, :, lanes(t)], lambda t: own[1, :, lanes(t)])

    def packet(r0, low, place, tile, state, steps):
        lanes = pl.ds(pl.multiple_of(tile * 128, 128), 128)
        tr = wave[r0 + 8, 0, :, lanes]
        ti = wave[r0 + 8, 1, :, lanes]
        after = []
        for n in range(steps):
            if n == 0:
                nr, ni = -TAN2 * tr, -TAN2 * ti
            else:
                dr, di = state[2 * n - 2], state[2 * n - 1]
                nr, ni = dr - TAN2 * tr, di - TAN2 * ti
                if n < steps - 1:
                    tr, ti = tr + dr, ti + di
            if n < 8:
                k = TABLE_OF_STEP[n]
                hr = tab[k, 0, tile, pl.ds(r0 + n + 8, 1), :]
                hi = tab[k, 1, tile, pl.ds(r0 + n + 8, 1), :]
                after += times(nr, ni, hr, hi)
        if steps == 9:
            raw[tile, place + r0 - low, 0] = nr
            raw[tile, place + r0 - low, 1] = ni
            inten = SCALE * SCALE * (nr * nr + ni * ni)
            row = r0 + 7
            off = pl.multiple_of((row % 4) * W + tile * 128, 128)
            if mode != "border":
                inten_out[row // 4, :, pl.ds(off, 128)] = inten
            elif low < 0:
                stage[(row + 24) // 4 % 6, :, pl.ds(off, 128)] = inten
            else:
                stage[row // 4 - 11, :, pl.ds(off, 128)] = inten
        return tuple(after)

    place = 0
    for low, count in PARTS[mode]:
        high = low + count + 15

        @pl.loop(0, TILES)
        def _(tile, low=low, high=high, count=count, place=place):
            @pl.loop(0, 2)
            def _(odd):
                top = high - odd
                if mode == "border" and low < 0:
                    state = tuple(state_in[2 * tile + odd, k] for k in range(16))
                    first = packet(0, low, place, tile, (), 1)
                    state = tuple(jnp.where(odd == 1, f, x) for f, x in zip(first, state[:2])) + state[2:]
                else:
                    state = ()
                    for i in range(8):
                        state = packet(top - 2 * i, low, place, tile, state, i + 1)
                group = 5 if count == 10 else 4

                def several(j, state):
                    for i in range(group):
                        state = packet(top - 16 - 2 * group * j - 2 * i, low, place, tile, state, 9)
                    return state

                state = lax.fori_loop(0, count // 2 // group, several, state)
                if mode == "inner":
                    for k in range(16):
                        state_out[2 * tile + odd, k] = state[k]

            if mode == "whole":
                pltpu.make_async_copy(raw.at[tile], raw_out.at[tile], sems.at[3 + tile]).start()

        place += count
    if mode == "border":
        stage[1, :, 3 * W : 4 * W] = inner_inten[1, :, 3 * W : 4 * W]
        stage[2, :, 0 : 3 * W] = inner_inten[13, :, 0 : 3 * W]
        departures += [
            pltpu.make_async_copy(stage.at[0:2], inten_out.at[0:2], sems.at[5]),
            pltpu.make_async_copy(stage.at[2:5], inten_out.at[13:16], sems.at[6]),
            pltpu.make_async_copy(raw, raw_out, sems.at[3]),
        ]
        for c in departures[-3:]:
            c.start()
    for c in departures:
        c.wait()
    if mode == "whole":
        for tile in range(TILES):
            pltpu.make_async_copy(raw.at[tile], raw_out.at[tile], sems.at[3 + tile]).wait()


def whole_block(shape):
    return pl.BlockSpec(shape, lambda i: (0,) * len(shape))


def sweep(mode, chunk, incident, phase, gauge, *more):
    total = sum(count for _, count in PARTS[mode])
    shapes = ((TILES, total, 2, 16, 128), (16, 16, 4 * W), (2, TILES, 88, 128))
    kept = ((5, 2, TILES, 88, 128), (81, 2, 16, W), (88, 2, 16, 128))
    f32 = lambda shape: jax.ShapeDtypeStruct(shape, jnp.float32)
    vmem, hbm = pl.BlockSpec(memory_space=pltpu.VMEM), pl.BlockSpec(memory_space=pltpu.HBM)
    outs = [pltpu.HBM(shapes[0], jnp.float32), f32(shapes[1]), pltpu.HBM(shapes[2], jnp.float32)]
    out_specs = [hbm, vmem, hbm]
    scratch = [pltpu.VMEM((3, TILES, 88, 128), jnp.float32), pltpu.VMEM(shapes[2], jnp.float32)]
    aliases = {}
    if mode == "border":
        ops = [phase, *more]
        in_specs = [vmem] * len(ops)
        aliases = {len(ops) - 3 + k: 4 + k for k in range(3)}
        outs = [pltpu.HBM(more[2].shape, jnp.float32), outs[0], pltpu.HBM(shapes[1], jnp.float32), outs[2]]
        out_specs = [hbm] * 4
        scratch += [pltpu.VMEM(shapes[0], jnp.float32), pltpu.VMEM((6, 16, 4 * W), jnp.float32)]
    else:
        ops = [phase, in_hbm(incident), gauge, *more]
        in_specs = [vmem, pl.BlockSpec(memory_space=pl.ANY)] + [vmem] * (1 + len(more))
        scratch.insert(0, pltpu.VMEM(incident.shape, jnp.float32))
    if mode == "whole":
        scratch = [pltpu.VMEM(x, jnp.float32) for x in kept] + scratch + [pltpu.VMEM(shapes[0], jnp.float32)]
    else:
        outs += [f32(x) for x in kept]
        out_specs += [vmem] * 3
    if mode == "inner":
        outs[0], out_specs[0] = f32(shapes[0]), vmem
        outs.append(f32((2 * TILES, 16, 16, 128)))
        out_specs.append(vmem)
    return pl.pallas_call(
        functools.partial(sweep_kernel, mode, chunk),
        out_shape=tuple(outs),
        in_specs=in_specs,
        out_specs=tuple(out_specs),
        scratch_shapes=scratch + [pltpu.SemaphoreType.DMA((7,))],
        input_output_aliases=aliases,
        compiler_params=pltpu.CompilerParams(vmem_limit_bytes=24 * 1024 * 1024),
        cost_estimate=pl.CostEstimate(flops=total * 16 * W * 120, bytes_accessed=8 * 1024 * 1024, transcendentals=0),
        name="sweep",
    )(*ops)


def merge_kernel(gauge_in, inner, border, whole, last_inner, last_border, last_whole, out, gauge):
    advance_gauge(gauge_in, gauge)

    def put(row, chunk, ref, at, last):
        er, ei = gauge[row + 1, 0], gauge[row + 1, 1]
        for t in range(TILES):
            fr, fi = (last[q, t, pl.ds(row + 9, 1), :] for q in range(2))
            tr, ti = times(ref[t, at, 0], ref[t, at, 1], fr, fi)
            off = pl.multiple_of(row * COLS + chunk * W + t * 128, 128)
            out[0, :, pl.ds(off, 128)] = tr * er + ti * ei
            out[1, :, pl.ds(off, 128)] = ti * er - tr * ei

    @pl.loop(0, 24)
    def _(j):
        for k in range(2):
            put(2 * j + k + 7, 0, inner, 2 * j + k, last_inner)

    for row in range(7):
        put(row, 0, border, row + 1, last_border)
    for row in range(55, 64):
        put(row, 0, border, row - 46, last_border)

    @pl.loop(0, 32)
    def _(j):
        for k in range(2):
            put(2 * j + k, 1, whole, 2 * j + k, last_whole)


def merge(gauge, raws, lasts, span):
    return pl.pallas_call(
        merge_kernel,
        grid=(1,),
        out_shape=jax.ShapeDtypeStruct((2, 16, span), jnp.float32),
        in_specs=[whole_block(x.shape) for x in (gauge, *raws, *lasts)],
        out_specs=whole_block((2, 16, span)),
        scratch_shapes=[pltpu.VMEM((88, 2, 16, 128), jnp.float32)],
        cost_estimate=pl.CostEstimate(flops=0, bytes_accessed=8 * 1024 * 1024, transcendentals=0),
        name="merge",
    )(gauge, *raws, *lasts)


def place_kernel(chunk, block, *refs):
    out, sems = refs[-2:]
    copies = []
    for b in range(16):
        for r in range(4):
            at = (4 * b + r) * COLS + chunk * W
            copies.append(pltpu.make_async_copy(block.at[b, :, r * W : r * W + W], out.at[:, at : at + W], sems.at[b, r]))
            copies[-1].start()
    for c in copies:
        c.wait()


def place(block, chunk, span, onto=None):
    hbm = pl.BlockSpec(memory_space=pl.ANY)
    ops = [block] if onto is None else [block, onto]
    return pl.pallas_call(
        functools.partial(place_kernel, chunk),
        out_shape=jax.ShapeDtypeStruct((16, span), jnp.float32),
        in_specs=[pl.BlockSpec(memory_space=pltpu.VMEM)] + [hbm] * (len(ops) - 1),
        out_specs=hbm,
        scratch_shapes=[pltpu.SemaphoreType.DMA((16, 4))],
        input_output_aliases={} if onto is None else {1: 0},
        compiler_params=pltpu.CompilerParams(vmem_limit_bytes=4 * 1024 * 1024),
        cost_estimate=pl.CostEstimate(flops=0, bytes_accessed=4 * 1024 * 1024, transcendentals=0),
        name="place",
    )(*ops)


def deconvolve(estimate, response, scaled, measured):
    for _ in range(ITERS):
        blurred = jnp.dot(response, estimate, precision=lax.Precision.HIGH, preferred_element_type=jnp.float32) + background
        projected = lax.dot_general(
            scaled,
            measured / blurred,
            (((0,), (0,)), ((), ())),
            precision=lax.Precision.HIGH,
            preferred_element_type=jnp.float32,
        )
        estimate = estimate * projected
    return estimate


def exchange(x):
    return lax.all_to_all(x, "ang", split_axis=0, concat_axis=0, tiled=True)


def on_device(incident, detuning, phase_table, response, counts):
    span = incident.shape[2]
    edges = pack(incident, phase_table)
    below, above = [], []
    for chunk in range(CHUNKS):
        lower, upper = edges[2 * chunk], edges[2 * chunk + 1]
        below.append(passed_along(lower, "lat", 1))
        above.append(passed_along(upper, "lat", -1))
    angle = -0.5 * detuning[None, :] * jnp.array([-10.0, -9.0, -8.0, -7.0, -6.0, -5.0, -4.0, -3.0, 8.0], jnp.float32)[:, None]
    gauge = jnp.stack([jnp.cos(angle), jnp.sin(angle)], axis=1)
    gauge = jnp.broadcast_to(gauge[..., None], gauge.shape + (128,))

    column_sums = jnp.sum(response, axis=0)
    scaled = response / column_sums[None, :]
    measured = [
        jnp.concatenate([counts[:, r * COLS + c * W : r * COLS + c * W + W] for r in range(4)], axis=1).astype(jnp.float32)
        for c in range(CHUNKS)
    ]

    raw_inner, inten_inner, last_inner, *kept, state = sweep("inner", 0, incident, phase_table, gauge)
    raw_inner, raw_border, inten0, last_border = sweep(
        "border", 0, None, phase_table, None, below[0], above[0], raw_inner, inten_inner, state, *kept
    )[:4]
    there0 = exchange(inten0)
    raw_whole, inten1, last_whole = sweep("whole", 1, incident, phase_table, gauge, below[1], above[1])
    there1 = exchange(inten1)
    estimate0 = deconvolve(there0.reshape(256, 4 * W), response, scaled, measured[0])
    back0 = exchange(estimate0.reshape(16, 16, 4 * W))
    there1, estimate0 = lax.optimization_barrier((there1, estimate0))
    estimate1 = deconvolve(there1.reshape(256, 4 * W), response, scaled, measured[1])
    back1 = exchange(estimate1.reshape(16, 16, 4 * W))
    exit_field = merge(gauge, (raw_inner, raw_border, raw_whole), (last_inner, last_border, last_whole), span)
    result = place(back0, 0, span)
    result = place(back1, 1, span, result)
    return exit_field, result


def solution(mesh):
    return jax.shard_map(
        on_device,
        mesh=mesh,
        in_specs=(P(None, "ang", "lat"), P("ang"), P(None, "lat"), P(), P(None, ("lat", "ang"))),
        out_specs=(P(None, "ang", "lat"), P("ang", "lat")),
        check_vma=False,
    )
```

```python
import functools
import math

import jax
import jax.numpy as jnp
from jax import lax
from jax.experimental import pallas as pl
from jax.experimental.pallas import tpu as pltpu
from jax.sharding import PartitionSpec as P


COLS = 512
ITERS = 6
W = 256
CHUNKS = COLS // W
TILES = W // 128
BELOW, ABOVE = 7, 9

coupling = 0.6
background = 0.25
TAN2 = math.tan(coupling) ** 2
SCALE = math.cos(coupling) ** 9 / math.tan(coupling)
TABLE_OF_STEP = (0, 0, 1, 2, 2, 3, 4, 4)


def passed_along(x, axis, by):
    devices = lax.axis_size(axis)
    return lax.ppermute(x, axis, [(i, (i + by) % devices) for i in range(devices)])


def turn(units):
    u = units * (1.0 / 32768.0)
    q = u * u
    half = math.pi / 2
    s = (-1) ** 5 * half**11 / math.factorial(11)
    for k in (4, 3, 2, 1, 0):
        s = s * q + (-1) ** k * half ** (2 * k + 1) / math.factorial(2 * k + 1)
    s = s * u
    c = half**12 / math.factorial(12)
    for k in (5, 4, 3, 2, 1, 0):
        c = c * q + (-1) ** k * half ** (2 * k) / math.factorial(2 * k)
    return 1.0 - 2.0 * s * s, 2.0 * s * c


def times(ar, ai, br, bi):
    return ar * br - ai * bi, ar * bi + ai * br


def in_hbm(x):
    return pltpu.with_memory_space_constraint(x, pltpu.HBM)


def pack_kernel(chunk, incident, phase, *refs):
    outs, edge, sems, edge_sems = refs[:2], refs[2], refs[3], refs[4]
    rows = incident.shape[2] // COLS
    sides = ((rows - BELOW, BELOW), (0, ABOVE))
    edges = [
        pltpu.make_async_copy(
            phase.at[:, first * COLS : (first + count) * COLS], edge.at[side, :, 0 : count * COLS], edge_sems.at[side]
        )
        for side, (first, count) in enumerate(sides)
    ]
    for c in edges:
        c.start()
    copies = []
    for side, (first, count) in enumerate(sides):
        for i in range(count):
            at = (first + i) * COLS + chunk * W
            for part in range(2):
                copies.append(
                    pltpu.make_async_copy(
                        incident.at[part, :, at : at + W],
                        outs[side].at[16 * part : 16 * part + 16, i * W : i * W + W],
                        sems.at[side, i, part],
                    )
                )
                copies[-1].start(priority=(i + part) % 2)
    for c in edges:
        c.wait()
    for side, (first, count) in enumerate(sides):
        for t in range(TILES):
            at = count * W + t * 128
            outs[side][:, at : at + 128] = jnp.zeros((32, 128), jnp.float32)
            for i in range(count):
                lane = i * COLS + chunk * W + t * 128
                outs[side][3 * i : 3 * i + 3, at : at + 128] = edge[side, :, lane : lane + 128].astype(jnp.float32)
    for c in copies:
        c.wait()


def pack(incident, phase, chunk):
    widths = [BELOW * W + TILES * 128, ABOVE * W + TILES * 128]
    return pl.pallas_call(
        functools.partial(pack_kernel, chunk),
        out_shape=tuple(jax.ShapeDtypeStruct((32, w), jnp.float32) for w in widths),
        in_specs=[pl.BlockSpec(memory_space=pl.ANY)] * 2,
        out_specs=(pl.BlockSpec(memory_space=pltpu.VMEM),) * 2,
        scratch_shapes=[
            pltpu.VMEM((2, 3, ABOVE * COLS), jnp.int32),
            pltpu.SemaphoreType.DMA((2, ABOVE, 2)),
            pltpu.SemaphoreType.DMA((2,)),
        ],
        compiler_params=pltpu.CompilerParams(vmem_limit_bytes=8 * 1024 * 1024),
        cost_estimate=pl.CostEstimate(flops=0, bytes_accessed=1024 * 1024, transcendentals=0),
        name="pack",
    )(in_hbm(incident), in_hbm(phase))


PARTS = {
    "inner": ((0, 48),),
    "border": ((-8, 8), (47, 10)),
    "whole": ((-7, 64),),
}
OWN_PHASES = {"inner": ((0, 64),), "border": ((0, 8), (48, 64)), "whole": ((0, 64),)}
TABLE_ROWS = {"inner": ((1, 9),), "border": ((0, 2), (8, 11)), "whole": ((0, 11),)}


def advance_gauge(gauge_in, gauge):
    step = gauge_in[8, 0], gauge_in[8, 1]
    strands = []
    for k in range(8):
        strands += [gauge_in[k, 0], gauge_in[k, 1]]
        gauge[k, 0] = strands[-2]
        gauge[k, 1] = strands[-1]

    def advance(i, strands):
        ahead = []
        for k in range(8):
            gr, gi = times(strands[2 * k], strands[2 * k + 1], *step)
            gauge[8 * i + 8 + k, 0] = gr
            gauge[8 * i + 8 + k, 1] = gi
            ahead += [gr, gi]
        return tuple(ahead)

    lax.fori_loop(0, 10, advance, tuple(strands))


def sweep_kernel(mode, chunk, phase, *refs):
    below = above = stage = state_out = None
    departures = []
    if mode == "border":
        below, above, inner_raw, inner_inten, state_in = refs[:5]
        inner_raw_out, raw_out, inten_out, last_out, tab, wave, gauge, phases, last, raw, stage, sems = refs[8:]
        departures = [
            pltpu.make_async_copy(inner_inten.at[2:13], inten_out.at[2:13], sems.at[0]),
            pltpu.make_async_copy(inner_raw, inner_raw_out, sems.at[1]),
        ]
        for c in departures:
            c.start()
    elif mode == "inner":
        incident, gauge_in, raw, inten_out, last_out, tab, wave, gauge, state_out, own, phases, last, sems = refs
    else:
        incident, gauge_in, below, above, raw_out, inten_out, last_out, tab, wave, gauge, own, phases, last, raw, sems = refs
    if mode != "border":
        half = incident.shape[2] // 2
        arrivals = [
            pltpu.make_async_copy(incident.at[:, :, k * half : k * half + half], own.at[:, :, k * half : k * half + half], sems.at[k])
            for k in range(2)
        ]
        for c in arrivals:
            c.start()
        advance_gauge(gauge_in, gauge)

    for t in range(TILES):
        for lo, hi in OWN_PHASES[mode]:
            for r in range(lo, hi):
                lane = r * COLS + chunk * W + t * 128
                units = phase[:, lane : lane + 128].astype(jnp.float32)
                for b in range(3):
                    phases[b, t, r + 8 : r + 9, :] = units[b : b + 1]
        if mode != "inner":
            for ref, count, first in ((below, BELOW, 1), (above, ABOVE, 72)):
                lanes = slice(count * W + t * 128, count * W + t * 128 + 128)
                for i in range(count):
                    for b in range(3):
                        phases[b, t, first + i : first + i + 1, :] = ref[3 * i + b : 3 * i + b + 1, lanes]

    top_row = lax.broadcasted_iota(jnp.int32, (8, 128), 0) == 0

    def tables(j, carried):
        at = pl.multiple_of(8 * j, 8)
        rolled = []
        for t in range(TILES):
            here, before = [], []
            for b in range(3):
                here.append(turn(phases[b, t, pl.ds(at, 8), :]))
                pair = []
                for q in range(2):
                    r = pltpu.roll(here[b][q], 1, 0)
                    pair.append(jnp.where(top_row, carried[(t * 3 + b) * 2 + q], r))
                    rolled.append(r)
                before.append(pair)
            for k, (a, b) in enumerate(((0, 0), (0, 1), (1, 1), (1, 2), (2, 2))):
                br, bi = before[b]
                ar, ai = here[a]
                tab[k, 0, t, pl.ds(at, 8), :] = ar * br + ai * bi
                tab[k, 1, t, pl.ds(at, 8), :] = ai * br - ar * bi
            last[0, t, pl.ds(at, 8), :] = SCALE * here[2][1]
            last[1, t, pl.ds(at, 8), :] = -SCALE * here[2][0]
        return tuple(rolled)

    for lo, hi in TABLE_ROWS[mode]:
        start = []
        for t in range(TILES):
            for b in range(3):
                if mode == "border" and lo > 0:
                    start += [pltpu.roll(x, 1, 0) for x in turn(phases[b, t, 8 * lo - 8 : 8 * lo, :])]
                else:
                    start += [jnp.zeros((8, 128), jnp.float32)] * 2
        lax.fori_loop(lo, hi, tables, tuple(start))
    departures.append(pltpu.make_async_copy(last, last_out, sems.at[2]))
    departures[-1].start()

    def regauge(row, re_of, im_of):
        er, ei = gauge[row + 10, 0], gauge[row + 10, 1]
        for t in range(TILES):
            tr, ti = times(re_of(t), im_of(t), er, ei)
            wave[row + 8, 0, :, t * 128 : t * 128 + 128] = tr
            wave[row + 8, 1, :, t * 128 : t * 128 + 128] = ti

    if mode != "inner":
        for ref, count, first in ((below, BELOW, -BELOW), (above, ABOVE, 64)):
            for i in range(count):
                lanes = lambda t, i=i: slice(i * W + t * 128, i * W + t * 128 + 128)
                regauge(first + i, lambda t, ref=ref: ref[0:16, lanes(t)], lambda t, ref=ref: ref[16:32, lanes(t)])
    if mode != "border":
        for c in arrivals:
            c.wait()

        @pl.loop(0, 16)
        def _(j):
            for k in range(4):
                row = 4 * j + k
                lanes = lambda t, row=row: pl.ds(pl.multiple_of(row * COLS + chunk * W + t * 128, 128), 128)
                regauge(row, lambda t: own[0, :, lanes(t)], lambda t: own[1, :, lanes(t)])

    def packet(r0, low, place, tile, state, steps):
        lanes = pl.ds(pl.multiple_of(tile * 128, 128), 128)
        tr = wave[r0 + 8, 0, :, lanes]
        ti = wave[r0 + 8, 1, :, lanes]
        after = []
        for n in range(steps):
            if n == 0:
                nr, ni = -TAN2 * tr, -TAN2 * ti
            else:
                dr, di = state[2 * n - 2], state[2 * n - 1]
                nr, ni = dr - TAN2 * tr, di - TAN2 * ti
                if n < steps - 1:
                    tr, ti = tr + dr, ti + di
            if n < 8:
                k = TABLE_OF_STEP[n]
                hr = tab[k, 0, tile, pl.ds(r0 + n + 8, 1), :]
                hi = tab[k, 1, tile, pl.ds(r0 + n + 8, 1), :]
                after += times(nr, ni, hr, hi)
        if steps == 9:
            raw[tile, place + r0 - low, 0] = nr
            raw[tile, place + r0 - low, 1] = ni
            inten = SCALE * SCALE * (nr * nr + ni * ni)
            row = r0 + 7
            off = pl.multiple_of((row % 4) * W + tile * 128, 128)
            if mode != "border":
                inten_out[row // 4, :, pl.ds(off, 128)] = inten
            elif low < 0:
                stage[(row + 24) // 4 % 6, :, pl.ds(off, 128)] = inten
            else:
                stage[row // 4 - 11, :, pl.ds(off, 128)] = inten
        return tuple(after)

    place = 0
    for low, count in PARTS[mode]:
        high = low + count + 15

        @pl.loop(0, TILES)
        def _(tile, low=low, high=high, count=count, place=place):
            @pl.loop(0, 2)
            def _(odd):
                top = high - odd
                if mode == "border" and low < 0:
                    state = tuple(state_in[2 * tile + odd, k] for k in range(16))
                    first = packet(0, low, place, tile, (), 1)
                    state = tuple(jnp.where(odd == 1, f, x) for f, x in zip(first, state[:2])) + state[2:]
                else:
                    state = ()
                    for i in range(8):
                        state = packet(top - 2 * i, low, place, tile, state, i + 1)
                group = 5 if count == 10 else 4

                def several(j, state):
                    for i in range(group):
                        state = packet(top - 16 - 2 * group * j - 2 * i, low, place, tile, state, 9)
                    return state

                state = lax.fori_loop(0, count // 2 // group, several, state)
                if mode == "inner":
                    for k in range(16):
                        state_out[2 * tile + odd, k] = state[k]

            if mode == "whole":
                pltpu.make_async_copy(raw.at[tile], raw_out.at[tile], sems.at[3 + tile]).start()

        place += count
    if mode == "border":
        stage[1, :, 3 * W : 4 * W] = inner_inten[1, :, 3 * W : 4 * W]
        stage[2, :, 0 : 3 * W] = inner_inten[13, :, 0 : 3 * W]
        departures += [
            pltpu.make_async_copy(stage.at[0:2], inten_out.at[0:2], sems.at[5]),
            pltpu.make_async_copy(stage.at[2:5], inten_out.at[13:16], sems.at[6]),
            pltpu.make_async_copy(raw, raw_out, sems.at[3]),
        ]
        for c in departures[-3:]:
            c.start()
    for c in departures:
        c.wait()
    if mode == "whole":
        for tile in range(TILES):
            pltpu.make_async_copy(raw.at[tile], raw_out.at[tile], sems.at[3 + tile]).wait()


def whole_block(shape):
    return pl.BlockSpec(shape, lambda i: (0,) * len(shape))


def sweep(mode, chunk, incident, phase, gauge, *more):
    total = sum(count for _, count in PARTS[mode])
    shapes = ((TILES, total, 2, 16, 128), (16, 16, 4 * W), (2, TILES, 88, 128))
    kept = ((5, 2, TILES, 88, 128), (81, 2, 16, W), (88, 2, 16, 128))
    f32 = lambda shape: jax.ShapeDtypeStruct(shape, jnp.float32)
    vmem, hbm = pl.BlockSpec(memory_space=pltpu.VMEM), pl.BlockSpec(memory_space=pltpu.HBM)
    outs = [pltpu.HBM(shapes[0], jnp.float32), f32(shapes[1]), pltpu.HBM(shapes[2], jnp.float32)]
    out_specs = [hbm, vmem, hbm]
    scratch = [pltpu.VMEM((3, TILES, 88, 128), jnp.float32), pltpu.VMEM(shapes[2], jnp.float32)]
    aliases = {}
    if mode == "border":
        ops = [phase, *more]
        in_specs = [vmem] * len(ops)
        aliases = {len(ops) - 3 + k: 4 + k for k in range(3)}
        outs = [pltpu.HBM(more[2].shape, jnp.float32), outs[0], pltpu.HBM(shapes[1], jnp.float32), outs[2]]
        out_specs = [hbm] * 4
        scratch += [pltpu.VMEM(shapes[0], jnp.float32), pltpu.VMEM((6, 16, 4 * W), jnp.float32)]
    else:
        ops = [phase, in_hbm(incident), gauge, *more]
        in_specs = [vmem, pl.BlockSpec(memory_space=pl.ANY)] + [vmem] * (1 + len(more))
        scratch.insert(0, pltpu.VMEM(incident.shape, jnp.float32))
    if mode == "whole":
        scratch = [pltpu.VMEM(x, jnp.float32) for x in kept] + scratch + [pltpu.VMEM(shapes[0], jnp.float32)]
    else:
        outs += [f32(x) for x in kept]
        out_specs += [vmem] * 3
    if mode == "inner":
        outs[0], out_specs[0] = f32(shapes[0]), vmem
        outs.append(f32((2 * TILES, 16, 16, 128)))
        out_specs.append(vmem)
    return pl.pallas_call(
        functools.partial(sweep_kernel, mode, chunk),
        out_shape=tuple(outs),
        in_specs=in_specs,
        out_specs=tuple(out_specs),
        scratch_shapes=scratch + [pltpu.SemaphoreType.DMA((7,))],
        input_output_aliases=aliases,
        compiler_params=pltpu.CompilerParams(vmem_limit_bytes=24 * 1024 * 1024),
        cost_estimate=pl.CostEstimate(flops=total * 16 * W * 120, bytes_accessed=8 * 1024 * 1024, transcendentals=0),
        name="sweep",
    )(*ops)


def merge_kernel(gauge_in, inner, border, whole, last_inner, last_border, last_whole, out, gauge):
    advance_gauge(gauge_in, gauge)

    def put(row, chunk, ref, at, last):
        er, ei = gauge[row + 1, 0], gauge[row + 1, 1]
        for t in range(TILES):
            fr, fi = (last[q, t, pl.ds(row + 9, 1), :] for q in range(2))
            tr, ti = times(ref[t, at, 0], ref[t, at, 1], fr, fi)
            off = pl.multiple_of(row * COLS + chunk * W + t * 128, 128)
            out[0, :, pl.ds(off, 128)] = tr * er + ti * ei
            out[1, :, pl.ds(off, 128)] = ti * er - tr * ei

    @pl.loop(0, 24)
    def _(j):
        for k in range(2):
            put(2 * j + k + 7, 0, inner, 2 * j + k, last_inner)

    for row in range(7):
        put(row, 0, border, row + 1, last_border)
    for row in range(55, 64):
        put(row, 0, border, row - 46, last_border)

    @pl.loop(0, 32)
    def _(j):
        for k in range(2):
            put(2 * j + k, 1, whole, 2 * j + k, last_whole)


def merge(gauge, raws, lasts, span):
    return pl.pallas_call(
        merge_kernel,
        grid=(1,),
        out_shape=jax.ShapeDtypeStruct((2, 16, span), jnp.float32),
        in_specs=[whole_block(x.shape) for x in (gauge, *raws, *lasts)],
        out_specs=whole_block((2, 16, span)),
        scratch_shapes=[pltpu.VMEM((88, 2, 16, 128), jnp.float32)],
        cost_estimate=pl.CostEstimate(flops=0, bytes_accessed=8 * 1024 * 1024, transcendentals=0),
        name="merge",
    )(gauge, *raws, *lasts)


def place_kernel(chunk, block, *refs):
    out, sems = refs[-2:]
    copies = []
    for b in range(16):
        for r in range(4):
            at = (4 * b + r) * COLS + chunk * W
            copies.append(pltpu.make_async_copy(block.at[b, :, r * W : r * W + W], out.at[:, at : at + W], sems.at[b, r]))
            copies[-1].start(priority=(b + r) % 2)
    for c in copies:
        c.wait()


def place(block, chunk, span, onto=None):
    hbm = pl.BlockSpec(memory_space=pl.ANY)
    ops = [block] if onto is None else [block, onto]
    return pl.pallas_call(
        functools.partial(place_kernel, chunk),
        out_shape=jax.ShapeDtypeStruct((16, span), jnp.float32),
        in_specs=[pl.BlockSpec(memory_space=pltpu.VMEM)] + [hbm] * (len(ops) - 1),
        out_specs=hbm,
        scratch_shapes=[pltpu.SemaphoreType.DMA((16, 4))],
        input_output_aliases={} if onto is None else {1: 0},
        compiler_params=pltpu.CompilerParams(vmem_limit_bytes=4 * 1024 * 1024),
        cost_estimate=pl.CostEstimate(flops=0, bytes_accessed=4 * 1024 * 1024, transcendentals=0),
        name="place",
    )(*ops)


def deconvolve(estimate, response, scaled, measured):
    for _ in range(ITERS):
        blurred = jnp.dot(response, estimate, precision=lax.Precision.HIGH, preferred_element_type=jnp.float32) + background
        projected = lax.dot_general(
            scaled,
            measured / blurred,
            (((0,), (0,)), ((), ())),
            precision=lax.Precision.HIGH,
            preferred_element_type=jnp.float32,
        )
        estimate = estimate * projected
    return estimate


def exchange(x):
    return lax.all_to_all(x, "ang", split_axis=0, concat_axis=0, tiled=True)


def on_device(incident, detuning, phase_table, response, counts):
    span = incident.shape[2]
    below, above = [], []
    for chunk in range(CHUNKS):
        lower, upper = pack(incident, phase_table, chunk)
        below.append(passed_along(lower, "lat", 1))
        above.append(passed_along(upper, "lat", -1))
    angle = -0.5 * detuning[None, :] * jnp.array([-10.0, -9.0, -8.0, -7.0, -6.0, -5.0, -4.0, -3.0, 8.0], jnp.float32)[:, None]
    gauge = jnp.stack([jnp.cos(angle), jnp.sin(angle)], axis=1)
    gauge = jnp.broadcast_to(gauge[..., None], gauge.shape + (128,))

    column_sums = jnp.sum(response, axis=0)
    scaled = response / column_sums[None, :]
    measured = [
        jnp.concatenate([counts[:, r * COLS + c * W : r * COLS + c * W + W] for r in range(4)], axis=1).astype(jnp.float32)
        for c in range(CHUNKS)
    ]

    raw_inner, inten_inner, last_inner, *kept, state = sweep("inner", 0, incident, phase_table, gauge)
    raw_inner, raw_border, inten0, last_border = sweep(
        "border", 0, None, phase_table, None, below[0], above[0], raw_inner, inten_inner, state, *kept
    )[:4]
    there0 = exchange(inten0)
    raw_whole, inten1, last_whole = sweep("whole", 1, incident, phase_table, gauge, below[1], above[1])
    there1 = exchange(inten1)
    estimate0 = deconvolve(there0.reshape(256, 4 * W), response, scaled, measured[0])
    back0 = exchange(estimate0.reshape(16, 16, 4 * W))
    there1, estimate0 = lax.optimization_barrier((there1, estimate0))
    estimate1 = deconvolve(there1.reshape(256, 4 * W), response, scaled, measured[1])
    back1 = exchange(estimate1.reshape(16, 16, 4 * W))
    exit_field = merge(gauge, (raw_inner, raw_border, raw_whole), (last_inner, last_border, last_whole), span)
    result = place(back0, 0, span)
    result = place(back1, 1, span, result)
    return exit_field, result


def solution(mesh):
    return jax.shard_map(
        on_device,
        mesh=mesh,
        in_specs=(P(None, "ang", "lat"), P("ang"), P(None, "lat"), P(), P(None, ("lat", "ang"))),
        out_specs=(P(None, "ang", "lat"), P("ang", "lat")),
        check_vma=False,
    )
```
